512 devices in a mesh: dp: 64 (over z_lo, y, core), mp: 8 (over x, z_hi).
Axes of the slice: x: 4, y: 8, z: 8 (z_hi: 2, z_lo: 4; z = z_hi * 4 + z_lo), core: 2. Of those that a mesh axis runs over, the one named last changes fastest.
Arguments:
- context: bfloat16 [65536, 2048], P('dp', 'mp'), may hold values from -6 to 6
- cotangent: bfloat16 [65536, 4096], P(('dp', 'mp')), may hold values from -24 to 24
- lengths: int32 [2048], P(('dp', 'mp')), may hold values from 1 to 32, as said below
- weight: float32 [2048, 4096], P('mp', 'dp'), may hold values from -0.125 to 0.125
- row_stat: float32 [2048], P('mp'), may hold values from 0.01 to 0.3
- col_stat: float32 [4096], P('dp'), may hold values from 0.01 to 0.3
Outputs:
- context_grad: bfloat16 [65536, 2048], P('dp', 'mp')
- update: float32 [2048, 4096], P('mp', 'dp')
- row_new: float32 [2048], P('mp')
- col_new: float32 [4096], P('dp')
The draws below stay inside these ranges and needn't reach their ends.
Inputs may be any that keep to these rules, and one draw needn't show every extreme that they name: The first lengths entry of each sequence's 32 slots are real tokens, the rest padding.
All inputs are finite; a program needn't handle non-finite values.
Results may differ from the reference program's by a relative error of at most 0.0049.
Values may be sent and summed in bfloat16 or wider, within the bound.
No kernel may reach another device: no remote copies, remote signals or barrier semaphores. Data moves between devices by JAX's collectives and lax.ppermute only.
A program may use at most 64 MiB of HBM per device.

```python
import math
import jax
import jax.numpy as jnp
from jax import lax

D = 4096
TGT_LEN = 32
INNER = 2048
TOKENS = 65536
SEQS = 2048
N_DP = 64


def draw_lengths(key, part):
    values = jax.random.randint(key, (SEQS,), 1, TGT_LEN + 1).astype(jnp.int32)
    return values.at[0].set(TGT_LEN)


def spiked(array, key, source, target, shards_of, factor):
    owner, partner = [(jnp.arange(array.shape[dim]) // (array.shape[dim] // shards_of)).reshape([-1 if axis == dim else 1 for axis in range(array.ndim)]) for dim in (source, target)]
    chosen = jax.random.permutation(key, shards_of)[partner]
    strong = (owner == chosen) | (owner == (partner + shards_of // 2) % shards_of)
    return jnp.where(strong, factor * array, array)


def block_levels(rng, shape, cuts, least, top_value):
    loudness, own = 1.0, jax.random.fold_in(rng, 6)
    for dim, parts in cuts:
        heights = jnp.exp(jax.random.uniform(jax.random.fold_in(own, dim), (parts,), jnp.float32, least / len(cuts), top_value / len(cuts)))
        loudness = loudness * jnp.repeat(heights, shape[dim] // parts).reshape([-1 if axis == dim else 1 for axis in range(len(shape))])
    return loudness


def normal_values(own_key, dims, width, most, split=(), held_as=jnp.bfloat16):
    drawn = width * jax.random.normal(own_key, dims, jnp.float32)
    if split:
        drawn = drawn * block_levels(own_key, dims, split, -0.22, 0.18)
    return jnp.clip(drawn, -most, most).astype(held_as)


def gaussian_with(rng, extent, deviation, bound, pieces, heavy, kind=jnp.bfloat16):
    values = deviation * jax.random.normal(rng, extent, jnp.float32)
    if pieces:
        values = values * block_levels(rng, extent, pieces, -0.22, 0.18)
    return jnp.clip(spiked(values, jax.random.fold_in(rng, 3), *heavy), -bound, bound).astype(kind)


def setup_inputs(seed: int = 0) -> dict:
    splits = jax.random.split(jax.random.key(seed), 7)
    return {
        "context": normal_values(splits[0], (TOKENS, INNER), 1.0, 6.0, ((0, 64), (1, 8))),
        "cotangent": gaussian_with(splits[1], (TOKENS, D), 1.0, 24.0, ((0, 512),), (0, 1, 512, 6.0)),
        "lengths": draw_lengths(jax.random.fold_in(splits[6], 71), 0),
        "weight": normal_values(splits[3], (INNER, D), INNER ** -0.5, 0.125, ((0, 8), (1, 64)), jnp.float32),
        "row_stat": jnp.clip(jnp.exp(math.log(0.3) - 3.4011974 * jax.random.uniform(splits[4], (INNER,), jnp.float32) ** block_levels(splits[4], (INNER,), ((0, 8),), -0.2, 0.2)), 0.01, 0.3),
        "col_stat": jnp.clip(jnp.exp(math.log(0.3) - 3.4011974 * jax.random.uniform(splits[5], (D,), jnp.float32) ** block_levels(splits[5], (D,), ((0, 64),), -0.2, 0.2)), 0.01, 0.3),
    }


decay_rate = 0.9
square_eps = 1e-30

def reference(context, cotangent, lengths, weight, row_stat, col_stat):
    seq_count = lengths.shape[0]
    position = jnp.arange(TGT_LEN, dtype=jnp.int32)
    inside = position[None, :] < lengths[:, None]
    shaped = cotangent.reshape(seq_count, TGT_LEN, D)
    masked = jnp.where(inside[:, :, None], shaped, jnp.zeros((), cotangent.dtype)).reshape(-1, D)
    weight_b = weight.astype(jnp.bfloat16)
    context_grad = jnp.dot(masked, weight_b.T, preferred_element_type=jnp.float32).astype(jnp.bfloat16)
    grad = jnp.dot(context.T, masked, preferred_element_type=jnp.float32) / N_DP
    square = grad * grad + square_eps
    row_new = decay_rate * row_stat + (1.0 - decay_rate) * lax.optimization_barrier(jnp.mean(square, axis=1))
    col_new = decay_rate * col_stat + (1.0 - decay_rate) * lax.optimization_barrier(jnp.mean(square, axis=0))
    raw_update = grad / jnp.sqrt(row_new[:, None] * col_new[None, :])
    update_rms = jnp.sqrt(jnp.mean(raw_update * raw_update))
    update = raw_update / jnp.maximum(1.0, update_rms)
    return (context_grad, update, row_new, col_new)
```

```python
import jax
import jax.numpy as jnp
from jax import lax
from jax.sharding import Mesh, PartitionSpec as P

decay_rate = 0.9
square_eps = 1e-30

SPLIT = (("zl", 4), ("y", 8), ("c", 2), ("x", 4), ("zh", 2))
SIZE = dict(SPLIT)
DP = ("zl", "y", "c")
MP = ("x", "zh")


def shift(value, axis, step):
    size = SIZE[axis]
    return lax.ppermute(value, axis, [(i, (i + step) % size) for i in range(size)])


def pick(value, index, axis=0):
    return lax.dynamic_index_in_dim(value, index, axis, keepdims=False)


def psum_each(value, axes):
    for axis in axes:
        value = lax.psum(value, axis)
    return value


def per_device(context, cotangent, lengths, weight, row_stat, col_stat):
    groups = SIZE["zl"] * SIZE["y"] * SIZE["c"]
    x, zh, y, c, zl = (lax.axis_index(a) for a in ("x", "zh", "y", "c", "zl"))
    seq_here = lengths.shape[0]
    tokens, width = cotangent.shape
    target_len = tokens // seq_here
    heads = context.shape[1]
    position = jnp.arange(target_len, dtype=jnp.int32)
    inside = position[None, :] < lengths[:, None]
    shaped = cotangent.reshape(seq_here, target_len, width)
    masked = jnp.where(inside[:, :, None], shaped, jnp.zeros((), cotangent.dtype)).reshape(
        tokens, width
    )
    weight_t = lax.all_gather(weight.T.astype(jnp.bfloat16), DP, axis=0, tiled=True)

    other = shift(masked, "zh", 1)
    steps = (1, 3, 2)
    blocks = [masked] + [shift(masked, "x", s) for s in steps]
    blocks += [other] + [shift(other, "x", s) for s in steps]
    gathered = jnp.concatenate(blocks, axis=0)
    places = [
        ((x - s) % SIZE["x"]) * SIZE["zh"] + (zh if half == 0 else 1 - zh)
        for half in range(2)
        for s in (0,) + steps
    ]
    ctx = context.reshape(SIZE["x"] * SIZE["zh"], tokens, heads)
    ctx = jnp.concatenate([pick(ctx, p) for p in places], axis=0)

    grad_t = lax.dot_general(
        gathered, ctx, (((0,), (0,)), ((), ())), preferred_element_type=jnp.float32
    )
    back = lax.dot_general(
        gathered, weight_t, (((1,), (0,)), ((), ())), preferred_element_type=jnp.float32
    ).astype(jnp.bfloat16)
    back = back.reshape(len(places), tokens, heads)
    context_grad = jnp.zeros_like(back)
    for i, p in enumerate(places):
        context_grad = lax.dynamic_update_index_in_dim(context_grad, back[i], p, 0)
    context_grad = context_grad.reshape(context.shape)

    cols = width // groups
    parts = grad_t.reshape(SIZE["zl"], SIZE["y"], SIZE["c"], cols, heads)
    parts = pick(parts, c, 2) + shift(pick(parts, 1 - c, 2), "c", 1)
    narrow = parts.astype(jnp.bfloat16)
    total = pick(parts, y, 1)
    for s in (1, 7, 2, 6, 3, 5, 4):
        total = total + shift(pick(narrow, (y + s) % SIZE["y"], 1), "y", s).astype(jnp.float32)
    part = pick(total, zl)
    for s in (1, 3, 2):
        part = part + shift(pick(total, (zl + s) % SIZE["zl"]), "zl", s)
    grad = part / groups

    square = grad * grad + square_eps
    inner_total = heads * SIZE["x"] * SIZE["zh"]
    col_all = psum_each(jnp.sum(square, axis=1), MP)
    col_new = decay_rate * col_stat + (1.0 - decay_rate) * (col_all / inner_total)
    scaled = grad * grad / col_new[:, None]
    row_all, row_scaled = psum_each(jnp.stack([jnp.sum(square, axis=0), jnp.sum(scaled, axis=0)]), DP)
    row_new = decay_rate * row_stat + (1.0 - decay_rate) * (row_all / width)
    square_sum = psum_each(jnp.sum(row_scaled / row_new), MP)
    raw_update = grad / jnp.sqrt(row_new[None, :] * col_new[:, None])
    update_rms = jnp.sqrt(square_sum / (inner_total * width))
    update = (raw_update / jnp.maximum(1.0, update_rms)).T
    return (context_grad, update, row_new, col_new)


def solution(mesh):
    names = tuple(name for name, _ in SPLIT)
    fine = Mesh(mesh.devices.reshape(tuple(size for _, size in SPLIT)), names)
    in_specs = (P(DP, MP), P(DP + MP, None), P(DP + MP), P(MP, DP), P(MP), P(DP))
    out_specs = (P(DP, MP), P(MP, DP), P(MP), P(DP))
    return jax.shard_map(
        per_device, mesh=fine, in_specs=in_specs, out_specs=out_specs, check_vma=False
    )
```

```python
import jax
import jax.numpy as jnp
from jax import lax
from jax.sharding import Mesh, PartitionSpec as P

decay_rate = 0.9
square_eps = 1e-30

SPLIT = (("zb", 2), ("za", 2), ("y", 8), ("c", 2), ("x", 4), ("zh", 2))
SIZE = dict(SPLIT)
DP = ("zb", "za", "y", "c")
MP = ("x", "zh")


def shift(value, axis, step):
    size = SIZE[axis]
    return lax.ppermute(value, axis, [(i, (i + step) % size) for i in range(size)])


def flip(value, axis, mask=1):
    return lax.ppermute(value, axis, [(i, i ^ mask) for i in range(SIZE[axis])])


def shift_zl(value, step):
    return lax.ppermute(value, ("zb", "za"), [(i, (i + step) % 4) for i in range(4)])


def turn(value, cross):
    to = {"swap": lambda a, b: (b, a), "right": lambda a, b: (b, 1 - a), "left": lambda a, b: (1 - b, a)}[cross]
    pairs = []
    for a in range(2):
        for b in range(2):
            p, q = to(a, b)
            pairs.append((2 * a + b, 2 * p + q))
    return lax.ppermute(value, ("zb", "zh"), pairs)


def pick(value, index, axis=0):
    return lax.dynamic_index_in_dim(value, index, axis, keepdims=False)


def ordered(bit, mine, other, axis=0):
    first = jnp.where(bit == 0, mine, other)
    second = jnp.where(bit == 0, other, mine)
    return jnp.stack([first, second], axis=axis)


def per_device(context, cotangent, lengths, weight, row_stat, col_stat):
    groups = SIZE["zb"] * SIZE["za"] * SIZE["y"] * SIZE["c"]
    zb, za, y, c, x, zh = (lax.axis_index(name) for name, _ in SPLIT)
    seq_here = lengths.shape[0]
    tokens, width = cotangent.shape
    target_len = tokens // seq_here
    heads = context.shape[1]
    half = width // 2
    cols = width // groups
    position = jnp.arange(target_len, dtype=jnp.int32)
    inside = position[None, :] < lengths[:, None]
    shaped = cotangent.reshape(seq_here, target_len, width)
    masked = jnp.where(inside[:, :, None], shaped, jnp.zeros((), cotangent.dtype)).reshape(
        tokens, width
    )

    theirs = flip(lax.dynamic_slice_in_dim(masked, (1 - zh) * half, half, 1), "zh")
    mine = lax.dynamic_slice_in_dim(masked, zh * half, half, 1)
    steps = (1, 3, 2)
    blocks = [(x, zh, mine)] + [((x - s) % SIZE["x"], zh, shift(mine, "x", s)) for s in steps]
    context_other = flip(context, "zh")
    blocks += [(x, 1 - zh, theirs)]
    blocks += [((x - s) % SIZE["x"], 1 - zh, shift(theirs, "x", s)) for s in steps]
    gathered = jnp.zeros((SIZE["x"], SIZE["zh"], tokens, half), masked.dtype)
    for px, pz, block in blocks:
        gathered = lax.dynamic_update_slice(gathered, block[None, None], (px, pz, 0, 0))
    gathered = gathered.reshape(-1, half)
    both = ordered(zh, context, context_other, 1).reshape(context.shape[0], 2 * heads)

    slim = weight.T.astype(jnp.bfloat16)
    w = ordered(zb, turn(slim, "swap"), turn(slim, "left"), 1).reshape(cols, 2 * heads)
    w = ordered(za, w, flip(w, "za"))[:, None]
    for bit in range(3):
        other = flip(w, "y", 1 << bit)
        w = ordered((y >> bit) & 1, w, other, 1)
        w = w.reshape((2, -1) + w.shape[3:])
    w = ordered(c, w, flip(w, "c"), 2).reshape(half, 2 * heads)

    grad_t = lax.dot_general(
        gathered, both, (((0,), (0,)), ((), ())), preferred_element_type=jnp.float32
    )
    back = lax.dot_general(
        gathered, w, (((1,), (0,)), ((), ())), preferred_element_type=jnp.float32
    )
    back_mine = lax.dynamic_slice_in_dim(back, zh * heads, heads, 1)
    back_theirs = lax.dynamic_slice_in_dim(back, (1 - zh) * heads, heads, 1).astype(jnp.bfloat16)
    context_grad = (back_mine + flip(back_theirs, "zh").astype(jnp.float32)).astype(jnp.bfloat16)

    parts = grad_t.reshape(SIZE["za"], SIZE["y"], SIZE["c"], cols, 2 * heads)
    parts = pick(parts, c, 2) + flip(pick(parts, 1 - c, 2), "c")
    narrow = parts.astype(jnp.bfloat16)
    total = pick(parts, y, 1)
    for s in (1, 7, 2, 6, 3, 5, 4):
        total = total + shift(pick(narrow, (y + s) % SIZE["y"], 1), "y", s).astype(jnp.float32)
    total = total.reshape(SIZE["za"], 2, cols // 2, 2 * heads)
    zl = zb * 2 + za

    def piece(i):
        return lax.dynamic_slice(total, (i % 2, i // 2, 0, 0), (1, 1) + total.shape[2:])[0, 0]

    part = piece(zl)
    for s in (1, 3, 2):
        part = part + shift_zl(piece((zl + s) % 4), s)
    grad = part / groups

    two = grad.reshape(cols // 2, 2, heads)
    grad_own = ordered(zh, turn(pick(two, zb, 1), "swap"), turn(pick(two, 1 - zb, 1), "right"))
    grad_own = grad_own.reshape(cols, heads)

    square = grad * grad + square_eps
    inner_total = heads * SIZE["x"] * SIZE["zh"]
    stat_here = turn(col_stat, "swap")
    stat_here = lax.dynamic_slice_in_dim(stat_here, zb * (cols // 2), cols // 2, 0)
    col_all = lax.psum(jnp.sum(square, axis=1), "x")
    col_here = decay_rate * stat_here + (1.0 - decay_rate) * (col_all / inner_total)
    scaled = grad * grad / col_here[:, None]
    rows = jnp.concatenate([jnp.sum(square, axis=0), jnp.sum(scaled, axis=0)])
    rows = lax.psum(lax.psum(rows, "c"), "y")
    slots = jnp.zeros((SIZE["zh"], SIZE["za"], SIZE["zb"], cols // 2), jnp.float32)
    slots = lax.dynamic_update_slice(slots, col_here[None, None, None], (zh, za, zb, 0))
    rows = lax.psum(jnp.concatenate([rows, slots.reshape(-1)]), ("zb", "za", "zh"))
    slots = rows[4 * heads :].reshape(slots.shape)
    col_new = lax.dynamic_slice(slots, (zb, za, 0, 0), (1, 1, 2, cols // 2)).reshape(cols)
    row_all = rows[: 2 * heads].reshape(2, heads)
    row_scaled = rows[2 * heads : 4 * heads].reshape(2, heads)
    stat_rows = jnp.stack([row_stat, flip(row_stat, "zh")])
    stat_rows = jnp.where(zh == 0, stat_rows, stat_rows[::-1])
    rows_new = decay_rate * stat_rows + (1.0 - decay_rate) * (row_all / width)
    square_sum = lax.psum(jnp.sum(row_scaled / rows_new), "x")
    row_new = pick(rows_new, zh)
    raw_update = grad_own / jnp.sqrt(row_new[None, :] * col_new[:, None])
    update_rms = jnp.sqrt(square_sum / (inner_total * width))
    update = (raw_update / jnp.maximum(1.0, update_rms)).T
    return (context_grad, update, row_new, col_new)


def solution(mesh):
    names = tuple(name for name, _ in SPLIT)
    fine = Mesh(mesh.devices.reshape(tuple(size for _, size in SPLIT)), names)
    in_specs = (P(DP, MP), P(DP + MP, None), P(DP + MP), P(MP, DP), P(MP), P(DP))
    out_specs = (P(DP, MP), P(MP, DP), P(MP), P(DP))
    return jax.shard_map(
        per_device, mesh=fine, in_specs=in_specs, out_specs=out_specs, check_vma=False
    )
```

```python
import jax
import jax.numpy as jnp
from jax import lax
from jax.experimental import pallas as pl
from jax.experimental.pallas import tpu as pltpu
from jax.sharding import Mesh, PartitionSpec as P


decay_rate = 0.9
square_eps = 1e-30

SPLIT = (("zb", 2), ("za", 2), ("y", 8), ("c", 2), ("x", 4), ("zh", 2))
SIZE = dict(SPLIT)
DP = ("zb", "za", "y", "c")
MP = ("x", "zh")
X_STEPS = (1, 3, 2)
Y_STEPS = (4, 3, 5, 2, 6, 1, 7)
Z_STEPS = (2, 1, 3)


def shift(value, axes, step):
    size = 4 if axes == ("zb", "za") else SIZE[axes]
    return lax.ppermute(value, axes, [(i, (i + step) % size) for i in range(size)])


def flip(value, axis, mask=1):
    return lax.ppermute(value, axis, [(i, i ^ mask) for i in range(SIZE[axis])])


def turn(value, to):
    pairs = []
    for a in range(2):
        for b in range(2):
            p, q = to(a, b)
            pairs.append((2 * a + b, 2 * p + q))
    return lax.ppermute(value, ("zb", "zh"), pairs)


def rotate(value, back):
    pairs = []
    for a in range(2):
        for b in range(2):
            for d in range(2):
                p, q, r = (b, d, a) if back else (d, a, b)
                pairs.append((4 * a + 2 * b + d, 4 * p + 2 * q + r))
    return lax.ppermute(value, ("zb", "c", "zh"), pairs)


def pick(value, index, axis=0):
    return lax.dynamic_index_in_dim(value, index, axis, keepdims=False)


def slot(value, index, count):
    here = lax.broadcasted_iota(jnp.int32, (count, 1), 0) == index
    return jnp.where(here, value[None], jnp.zeros((), value.dtype)).reshape(-1)


def arrange_kernel(info_ref, own_ref, other_ref, out_ref):
    count, tokens, heads = own_ref.shape
    own_at = pl.multiple_of(info_ref[count] * heads, heads)
    other_at = pl.multiple_of((1 - info_ref[count]) * heads, heads)
    for i in range(count):
        at = info_ref[i]
        span = slice(i * tokens, (i + 1) * tokens)
        out_ref[pl.ds(own_at, heads), span] = own_ref[at].T
        out_ref[pl.ds(other_at, heads), span] = other_ref[at].T


def grad_kernel(ctx_ref, *refs):
    blocks, (keep_ref, send_ref) = refs[:-2], refs[-2:]
    tile = jnp.concatenate([ref[...] for ref in blocks], axis=0)
    got = jnp.dot(ctx_ref[...], tile, preferred_element_type=jnp.float32)
    rows = keep_ref.shape[2]
    for k in range(2):
        span = slice(k * 128, (k + 1) * 128)
        send_ref[k, 0] = got[:rows, span].astype(send_ref.dtype)
        keep_ref[k, 0] = got[rows:, span]


def back_kernel(info_ref, a0_ref, a1_ref, b0_ref, b1_ref, *refs):
    blocks, (own_ref, other_ref, acc_ref) = refs[:-3], refs[-3:]
    count, tokens, heads = own_ref.shape
    step = pl.program_id(0)
    first = info_ref[count + 3] == 0
    rows = []
    for a_ref, b_ref in ((a0_ref, b0_ref), (a1_ref, b1_ref)):
        mine, came = a_ref[0], b_ref[0]
        rows += [jnp.where(first, mine, came), jnp.where(first, came, mine)]
    tile = jnp.concatenate([ref[...] for ref in blocks], axis=0)
    got = jnp.dot(tile, jnp.concatenate(rows, axis=0), preferred_element_type=jnp.float32)

    @pl.when(step == 0)
    def _():
        acc_ref[...] = got

    @pl.when(step > 0)
    def _():
        acc_ref[...] += got

    @pl.when(step == pl.num_programs(0) - 1)
    def _():
        straight = info_ref[count + 4] == 0
        for i in range(count):
            at = info_ref[i]
            left = acc_ref[i * tokens : (i + 1) * tokens, :heads]
            right = acc_ref[i * tokens : (i + 1) * tokens, heads:]
            own_ref[at] = jnp.where(straight, left, right)
            other_ref[at] = jnp.where(straight, right, left).astype(other_ref.dtype)


def total_kernel(mine_ref, *refs):
    came, out_ref = refs[:-1], refs[-1]
    cols = out_ref.shape[1]
    for za in range(2):
        total = mine_ref[za]
        for ref in came:
            total = total + ref[za].astype(jnp.float32)
        turned = total.T
        for zb in range(2):
            out_ref[2 * zb + za] = turned[zb * cols : (zb + 1) * cols]


def arrange(info, own, other):
    count, tokens, heads = own.shape
    full = pl.BlockSpec(own.shape, lambda i, p: (0, 0, 0))
    return pl.pallas_call(
        arrange_kernel,
        grid_spec=pltpu.PrefetchScalarGridSpec(
            num_scalar_prefetch=1,
            grid=(1,),
            in_specs=[full, full],
            out_specs=pl.BlockSpec((2 * heads, count * tokens), lambda i, p: (0, 0)),
        ),
        out_shape=jax.ShapeDtypeStruct((2 * heads, count * tokens), own.dtype),
        name="arrange",
    )(info, own, other)


def grad_of(ctx, blocks):
    twice, rows_in = ctx.shape
    tokens, half = blocks[0].shape
    tile = 256
    per_za = half // SIZE["za"] // tile
    shape = (SIZE["y"], SIZE["za"], twice // 2, 128)
    out = pl.BlockSpec((2, 1) + shape[2:], lambda t: (t % per_za, t // per_za, 0, 0))
    return pl.pallas_call(
        grad_kernel,
        grid=(half // tile,),
        in_specs=[pl.BlockSpec(ctx.shape, lambda t: (0, 0))]
        + [pl.BlockSpec((tokens, tile), lambda t: (0, t))] * len(blocks),
        out_specs=[out, out],
        out_shape=[
            jax.ShapeDtypeStruct(shape, jnp.float32),
            jax.ShapeDtypeStruct(shape, jnp.bfloat16),
        ],
        cost_estimate=pl.CostEstimate(
            flops=2 * twice * rows_in * half, transcendentals=0, bytes_accessed=9 << 20
        ),
        name="grad",
    )(ctx, *blocks)


def back_of(info, mine, came, blocks):
    _, cols, twice = mine.shape
    tokens, half = blocks[0].shape
    count = len(blocks)
    tile = 4 * cols
    per_za = half // SIZE["za"] // tile
    shape = (count, tokens, twice // 2)
    full = pl.BlockSpec(shape, lambda k, p: (0, 0, 0))

    def weights(low):
        def index(k, p):
            z = (k // per_za) ^ p[count + 1]
            y = ((k % per_za) * 2 + low) ^ p[count + 2]
            return ((y & 1) * 8 + ((y >> 1) & 1) * 4 + ((y >> 2) & 1) * 2 + z, 0, 0)

        return pl.BlockSpec((1, cols, twice), index)

    return pl.pallas_call(
        back_kernel,
        grid_spec=pltpu.PrefetchScalarGridSpec(
            num_scalar_prefetch=1,
            grid=(half // tile,),
            in_specs=[weights(0), weights(1), weights(0), weights(1)]
            + [pl.BlockSpec((tokens, tile), lambda k, p: (0, k))] * count,
            out_specs=[full, full],
            scratch_shapes=[pltpu.VMEM((count * tokens, twice), jnp.float32)],
        ),
        out_shape=[
            jax.ShapeDtypeStruct(shape, jnp.float32),
            jax.ShapeDtypeStruct(shape, jnp.bfloat16),
        ],
        cost_estimate=pl.CostEstimate(
            flops=2 * twice * count * tokens * half, transcendentals=0, bytes_accessed=8 << 20
        ),
        name="back",
    )(info, mine, mine, came, came, *blocks)


def total_of(mine, came, cols):
    return pl.pallas_call(
        total_kernel,
        out_shape=jax.ShapeDtypeStruct((4, cols, mine.shape[1]), jnp.float32),
        name="total",
    )(mine, *came)


def per_device(context, cotangent, lengths, weight, row_stat, col_stat):
    groups = SIZE["zb"] * SIZE["za"] * SIZE["y"] * SIZE["c"]
    zb, za, y, c, x, zh = (lax.axis_index(name) for name, _ in SPLIT)
    seq_here = lengths.shape[0]
    tokens, width = cotangent.shape
    target_len = tokens // seq_here
    heads = context.shape[1]
    half = width // 2
    cols = width // groups
    position = jnp.arange(target_len, dtype=jnp.int32)
    inside = position[None, :] < lengths[:, None]
    shaped = cotangent.reshape(seq_here, target_len, width)
    masked = jnp.where(inside[:, :, None], shaped, jnp.zeros((), cotangent.dtype)).reshape(
        tokens, width
    )

    left, right = masked[:, :half], masked[:, half:]
    theirs = flip(jnp.where(zh == 0, right, left), "zh")
    mine = jnp.where(zh == 0, left, right)
    blocks = [mine] + [shift(mine, "x", s) for s in X_STEPS]
    blocks += [theirs] + [shift(theirs, "x", s) for s in X_STEPS]
    info = [((x - s) & (SIZE["x"] - 1)) * 2 + z for z in (zh, 1 - zh) for s in (0,) + X_STEPS]
    info = jnp.stack(info + [1 - (c ^ zh), za, y, c, zb ^ zh]).astype(jnp.int32)
    context_other = flip(context, "zh")
    by_block = (len(blocks), tokens, heads)
    ctx = arrange(info, context.reshape(by_block), context_other.reshape(by_block))

    slim = weight.T.astype(jnp.bfloat16)
    w_a = turn(slim, lambda a, b: (b, a))
    w_b = turn(slim, lambda a, b: (1 - b, a))
    w = jnp.concatenate([w_a, w_b], axis=1)[None]
    w = jnp.concatenate([w, flip(w, "za")], axis=0)
    for bit in (2, 1, 0):
        w = jnp.concatenate([w, flip(w, "y", 1 << bit)], axis=0)
    w_came = flip(w, "c")

    stats = rotate(jnp.concatenate([row_stat, col_stat]), True)
    row_held, col_held = stats[:heads], stats[heads:]

    kept, sent = grad_of(ctx, blocks)
    parts = kept + flip(sent, "c").astype(jnp.float32)

    own, other = back_of(info, w, w_came, blocks)
    context_grad = (own + flip(other, "zh").astype(jnp.float32)).astype(jnp.bfloat16)
    context_grad = context_grad.reshape(context.shape)

    narrow = parts.astype(jnp.bfloat16)
    last = SIZE["y"] - 1
    came = [shift(pick(narrow, (y + s) & last), "y", s) for s in Y_STEPS]
    pieces = total_of(pick(parts, y), came, cols)
    zl = zb * 2 + za
    part = pick(pieces, zl)
    for s in Z_STEPS:
        part = part + shift(pick(pieces, (zl + s) & 3), ("zb", "za"), s)
    grad = part / groups
    grad_own = rotate(grad, False)

    square = grad * grad + square_eps
    inner_total = heads * SIZE["x"] * SIZE["zh"]
    col_all = lax.psum(jnp.sum(square, axis=1), "c")
    col_all = lax.psum(col_all, "x")
    col_here = decay_rate * col_held + (1.0 - decay_rate) * (col_all / inner_total)
    scaled = grad * grad / col_here[:, None]
    rows = jnp.concatenate([jnp.sum(square, axis=0), jnp.sum(scaled, axis=0)])
    rows = lax.psum(rows, "y")
    rows = lax.psum(jnp.concatenate([rows, slot(col_here, zl, 4)]), ("zb", "za"))
    slots = slot(rows[2 * heads :], zh, 2)
    rows = lax.psum(jnp.concatenate([rows[: 2 * heads], slots]), "zh")
    slots = rows[2 * heads :].reshape(8, cols)
    col_new = pick(slots, zb * 4 + c * 2 + za)
    row_here = decay_rate * row_held + (1.0 - decay_rate) * (rows[:heads] / width)
    square_sum = jnp.sum(rows[heads : 2 * heads] / row_here)
    tail = jnp.broadcast_to(square_sum, (128,))
    sums = lax.psum(jnp.concatenate([slot(row_here, c, 2), tail]), "c")
    row_new = pick(sums[: 2 * heads].reshape(2, heads), zh)
    square_sum = lax.psum(sums[2 * heads], "x")
    raw_update = grad_own / jnp.sqrt(row_new[None, :] * col_new[:, None])
    update_rms = jnp.sqrt(square_sum / (inner_total * width))
    update = (raw_update / jnp.maximum(1.0, update_rms)).T
    return (context_grad, update, row_new, col_new)


def solution(mesh):
    names = tuple(name for name, _ in SPLIT)
    fine = Mesh(mesh.devices.reshape(tuple(size for _, size in SPLIT)), names)
    in_specs = (P(DP, MP), P(DP + MP, None), P(DP + MP), P(MP, DP), P(MP), P(DP))
    out_specs = (P(DP, MP), P(MP, DP), P(MP), P(DP))
    return jax.shard_map(
        per_device, mesh=fine, in_specs=in_specs, out_specs=out_specs, check_vma=False
    )
```

```python
import jax
import jax.numpy as jnp
from jax import lax
from jax.experimental import pallas as pl
from jax.experimental.pallas import tpu as pltpu
from jax.sharding import Mesh, PartitionSpec as P


decay_rate = 0.9
square_eps = 1e-30

SPLIT = (("zb", 2), ("za", 2), ("y", 8), ("c", 2), ("x", 4), ("zh", 2))
SIZE = dict(SPLIT)
DP = ("zb", "za", "y", "c")
MP = ("x", "zh")
X_STEPS = (1, 3, 2)
Y_STEPS = (4, 3, 5, 2, 6, 1, 7)
Z_STEPS = (2, 1, 3)


def shift(value, axes, step):
    size = 4 if axes == ("zb", "za") else SIZE[axes]
    return lax.ppermute(value, axes, [(i, (i + step) % size) for i in range(size)])


def flip(value, axis, mask=1):
    return lax.ppermute(value, axis, [(i, i ^ mask) for i in range(SIZE[axis])])


def turn(value, to):
    pairs = []
    for a in range(2):
        for b in range(2):
            p, q = to(a, b)
            pairs.append((2 * a + b, 2 * p + q))
    return lax.ppermute(value, ("zb", "zh"), pairs)


def rotate(value, back):
    pairs = []
    for a in range(2):
        for b in range(2):
            for d in range(2):
                p, q, r = (b, d, a) if back else (d, a, b)
                pairs.append((4 * a + 2 * b + d, 4 * p + 2 * q + r))
    return lax.ppermute(value, ("zb", "c", "zh"), pairs)


def pick(value, index, axis=0):
    return lax.dynamic_index_in_dim(value, index, axis, keepdims=False)


def slot(value, index, count):
    here = lax.broadcasted_iota(jnp.int32, (count, 1), 0) == index
    return jnp.where(here, value[None], jnp.zeros((), value.dtype)).reshape(-1)


def arrange_kernel(info_ref, own_ref, other_ref, out_ref):
    count, tokens, heads = own_ref.shape
    own_at = pl.multiple_of(info_ref[count] * heads, heads)
    other_at = pl.multiple_of((1 - info_ref[count]) * heads, heads)
    for i in range(count):
        at = info_ref[i]
        span = slice(i * tokens, (i + 1) * tokens)
        out_ref[pl.ds(own_at, heads), span] = own_ref[at].T
        out_ref[pl.ds(other_at, heads), span] = other_ref[at].T


def grad_kernel(ctx_ref, *refs):
    blocks, (keep_ref, send_ref) = refs[:-2], refs[-2:]
    tile = jnp.concatenate([ref[...] for ref in blocks], axis=0)
    got = jnp.dot(ctx_ref[...], tile, preferred_element_type=jnp.float32)
    rows, cols = keep_ref.shape[2:]
    for k in range(keep_ref.shape[0]):
        span = slice(k * cols, (k + 1) * cols)
        send_ref[k, 0] = got[:rows, span].astype(send_ref.dtype)
        keep_ref[k, 0] = got[rows:, span]


def back_kernel(info_ref, *refs):
    y_count = SIZE["y"]
    mine_refs, came_refs = refs[:y_count], refs[y_count : 2 * y_count]
    blocks, (own_ref, other_ref, acc_ref) = refs[2 * y_count : -3], refs[-3:]
    count, tokens, heads = own_ref.shape
    step = pl.program_id(0)
    first = info_ref[count + 3] == 0
    rows = []
    for mine_ref, came_ref in zip(mine_refs, came_refs):
        mine, came = mine_ref[0], came_ref[0]
        rows += [jnp.where(first, mine, came), jnp.where(first, came, mine)]
    tile = jnp.concatenate([ref[...] for ref in blocks], axis=0)
    got = jnp.dot(tile, jnp.concatenate(rows, axis=0), preferred_element_type=jnp.float32)

    @pl.when(step == 0)
    def _():
        acc_ref[...] = got

    @pl.when(step > 0)
    def _():
        acc_ref[...] += got

    @pl.when(step == pl.num_programs(0) - 1)
    def _():
        straight = info_ref[count + 4] == 0
        for i in range(count):
            at = info_ref[i]
            left = acc_ref[i * tokens : (i + 1) * tokens, :heads]
            right = acc_ref[i * tokens : (i + 1) * tokens, heads:]
            own_ref[at] = jnp.where(straight, left, right)
            other_ref[at] = jnp.where(straight, right, left).astype(other_ref.dtype)


def total_kernel(mine_ref, *refs):
    came, out_ref = refs[:-1], refs[-1]
    cols = out_ref.shape[1]
    for za in range(2):
        total = mine_ref[za]
        for ref in came:
            total = total + ref[za].astype(jnp.float32)
        turned = total.T
        for zb in range(2):
            out_ref[2 * zb + za] = turned[zb * cols : (zb + 1) * cols]


def arrange(info, own, other):
    count, tokens, heads = own.shape
    full = pl.BlockSpec(own.shape, lambda i, p: (0, 0, 0))
    return pl.pallas_call(
        arrange_kernel,
        grid_spec=pltpu.PrefetchScalarGridSpec(
            num_scalar_prefetch=1,
            grid=(1,),
            in_specs=[full, full],
            out_specs=pl.BlockSpec((2 * heads, count * tokens), lambda i, p: (0, 0)),
        ),
        out_shape=jax.ShapeDtypeStruct((2 * heads, count * tokens), own.dtype),
        name="arrange",
    )(info, own, other)


def grad_of(ctx, blocks):
    twice, rows_in = ctx.shape
    tokens, half = blocks[0].shape
    tile = half // SIZE["za"]
    shape = (SIZE["y"], SIZE["za"], twice // 2, tile // SIZE["y"])
    out = pl.BlockSpec((SIZE["y"], 1) + shape[2:], lambda t: (0, t, 0, 0))
    return pl.pallas_call(
        grad_kernel,
        grid=(half // tile,),
        in_specs=[pl.BlockSpec(ctx.shape, lambda t: (0, 0))]
        + [pl.BlockSpec((tokens, tile), lambda t: (0, t))] * len(blocks),
        out_specs=[out, out],
        out_shape=[
            jax.ShapeDtypeStruct(shape, jnp.float32),
            jax.ShapeDtypeStruct(shape, jnp.bfloat16),
        ],
        cost_estimate=pl.CostEstimate(
            flops=2 * twice * rows_in * half, transcendentals=0, bytes_accessed=9 << 20
        ),
        name="grad",
    )(ctx, *blocks)


def back_of(info, mine, came, blocks):
    _, cols, twice = mine.shape
    tokens, half = blocks[0].shape
    count = len(blocks)
    tile = half // SIZE["za"]
    shape = (count, tokens, twice // 2)
    full = pl.BlockSpec(shape, lambda k, p: (0, 0, 0))

    def weights(place):
        def index(k, p):
            z = k ^ p[count + 1]
            y = place ^ p[count + 2]
            return ((y & 1) * 8 + ((y >> 1) & 1) * 4 + ((y >> 2) & 1) * 2 + z, 0, 0)

        return pl.BlockSpec((1, cols, twice), index)

    return pl.pallas_call(
        back_kernel,
        grid_spec=pltpu.PrefetchScalarGridSpec(
            num_scalar_prefetch=1,
            grid=(half // tile,),
            in_specs=[weights(y) for y in range(SIZE["y"])] * 2
            + [pl.BlockSpec((tokens, tile), lambda k, p: (0, k))] * count,
            out_specs=[full, full],
            scratch_shapes=[pltpu.VMEM((count * tokens, twice), jnp.float32)],
        ),
        out_shape=[
            jax.ShapeDtypeStruct(shape, jnp.float32),
            jax.ShapeDtypeStruct(shape, jnp.bfloat16),
        ],
        cost_estimate=pl.CostEstimate(
            flops=2 * twice * count * tokens * half, transcendentals=0, bytes_accessed=8 << 20
        ),
        name="back",
    )(info, *([mine] * SIZE["y"] + [came] * SIZE["y"]), *blocks)


def total_of(mine, came, cols):
    return pl.pallas_call(
        total_kernel,
        out_shape=jax.ShapeDtypeStruct((4, cols, mine.shape[1]), jnp.float32),
        name="total",
    )(mine, *came)


def per_device(context, cotangent, lengths, weight, row_stat, col_stat):
    groups = SIZE["zb"] * SIZE["za"] * SIZE["y"] * SIZE["c"]
    zb, za, y, c, x, zh = (lax.axis_index(name) for name, _ in SPLIT)
    seq_here = lengths.shape[0]
    tokens, width = cotangent.shape
    target_len = tokens // seq_here
    heads = context.shape[1]
    half = width // 2
    cols = width // groups
    position = jnp.arange(target_len, dtype=jnp.int32)
    inside = position[None, :] < lengths[:, None]
    shaped = cotangent.reshape(seq_here, target_len, width)
    masked = jnp.where(inside[:, :, None], shaped, jnp.zeros((), cotangent.dtype)).reshape(
        tokens, width
    )

    left, right = masked[:, :half], masked[:, half:]
    theirs = flip(jnp.where(zh == 0, right, left), "zh")
    mine = jnp.where(zh == 0, left, right)
    blocks = [mine] + [shift(mine, "x", s) for s in X_STEPS]
    blocks += [theirs] + [shift(theirs, "x", s) for s in X_STEPS]
    info = [((x - s) & (SIZE["x"] - 1)) * 2 + z for z in (zh, 1 - zh) for s in (0,) + X_STEPS]
    info = jnp.stack(info + [1 - (c ^ zh), za, y, c, zb ^ zh]).astype(jnp.int32)
    context_other = flip(context, "zh")
    by_block = (len(blocks), tokens, heads)
    ctx = arrange(info, context.reshape(by_block), context_other.reshape(by_block))

    slim = weight.T.astype(jnp.bfloat16)
    w_a = turn(slim, lambda a, b: (b, a))
    w_b = turn(slim, lambda a, b: (1 - b, a))
    w = jnp.concatenate([w_a, w_b], axis=1)[None]
    w = jnp.concatenate([w, flip(w, "za")], axis=0)
    for bit in (2, 1, 0):
        other = flip(w, "y", 1 << bit)
        w = jnp.concatenate([w, other], axis=0)
    w_came = flip(w, "c")

    stats = rotate(jnp.concatenate([row_stat, col_stat]), True)
    row_held, col_held = stats[:heads], stats[heads:]

    kept, sent = grad_of(ctx, blocks)
    parts = kept + flip(sent, "c").astype(jnp.float32)

    own, other = back_of(info, w, w_came, blocks)
    context_grad = (own + flip(other, "zh").astype(jnp.float32)).astype(jnp.bfloat16)
    context_grad = context_grad.reshape(context.shape)

    narrow = parts.astype(jnp.bfloat16)
    last = SIZE["y"] - 1
    came = [shift(pick(narrow, (y + s) & last), "y", s) for s in Y_STEPS]
    pieces = total_of(pick(parts, y), came, cols)
    zl = zb * 2 + za
    part = pick(pieces, zl)
    for s in Z_STEPS:
        part = part + shift(pick(pieces, (zl + s) & 3), ("zb", "za"), s)
    grad = part / groups
    grad_own = rotate(grad, False)

    square = grad * grad + square_eps
    inner_total = heads * SIZE["x"] * SIZE["zh"]
    col_all = lax.psum(jnp.sum(square, axis=1), "c")
    col_all = lax.psum(col_all, "x")
    col_here = decay_rate * col_held + (1.0 - decay_rate) * (col_all / inner_total)
    scaled = grad * grad / col_here[:, None]
    rows = jnp.concatenate([jnp.sum(square, axis=0), jnp.sum(scaled, axis=0)])
    rows = lax.psum(rows, "y")
    rows = lax.psum(jnp.concatenate([rows, slot(col_here, zl, 4)]), ("zb", "za"))
    slots = slot(rows[2 * heads :], zh, 2)
    rows = lax.psum(jnp.concatenate([rows[: 2 * heads], slots]), "zh")
    slots = rows[2 * heads :].reshape(8, cols)
    col_new = pick(slots, zb * 4 + c * 2 + za)
    row_here = decay_rate * row_held + (1.0 - decay_rate) * (rows[:heads] / width)
    square_sum = jnp.sum(rows[heads : 2 * heads] / row_here)
    tail = jnp.broadcast_to(square_sum, (128,))
    sums = lax.psum(jnp.concatenate([slot(row_here, c, 2), tail]), "c")
    row_new = pick(sums[: 2 * heads].reshape(2, heads), zh)
    square_sum = lax.psum(sums[2 * heads], "x")
    raw_update = grad_own / jnp.sqrt(row_new[None, :] * col_new[:, None])
    update_rms = jnp.sqrt(square_sum / (inner_total * width))
    update = (raw_update / jnp.maximum(1.0, update_rms)).T
    return (context_grad, update, row_new, col_new)


def solution(mesh):
    names = tuple(name for name, _ in SPLIT)
    fine = Mesh(mesh.devices.reshape(tuple(size for _, size in SPLIT)), names)
    in_specs = (P(DP, MP), P(DP + MP, None), P(DP + MP), P(MP, DP), P(MP), P(DP))
    out_specs = (P(DP, MP), P(MP, DP), P(MP), P(DP))
    return jax.shard_map(
        per_device, mesh=fine, in_specs=in_specs, out_specs=out_specs, check_vma=False
    )
```

```python
import jax
import jax.numpy as jnp
from jax import lax
from jax.experimental import pallas as pl
from jax.experimental.pallas import tpu as pltpu
from jax.sharding import Mesh, PartitionSpec as P


decay_rate = 0.9
square_eps = 1e-30

SPLIT = (("zb", 2), ("za", 2), ("y", 8), ("c", 2), ("x", 4), ("zh", 2))
SIZE = dict(SPLIT)
DP = ("zb", "za", "y", "c")
MP = ("x", "zh")
X_STEPS = (1, 3, 2)
Y_STEPS = (4, 3, 5, 2, 6, 1, 7)
Z_STEPS = (2, 1, 3)


def shift(value, axes, step):
    size = 4 if axes == ("zb", "za") else SIZE[axes]
    return lax.ppermute(value, axes, [(i, (i + step) % size) for i in range(size)])


def flip(value, axis, mask=1):
    return lax.ppermute(value, axis, [(i, i ^ mask) for i in range(SIZE[axis])])


def turn(value, to):
    pairs = []
    for a in range(2):
        for b in range(2):
            p, q = to(a, b)
            pairs.append((2 * a + b, 2 * p + q))
    return lax.ppermute(value, ("zb", "zh"), pairs)


def rotate(value, back):
    pairs = []
    for a in range(2):
        for b in range(2):
            for d in range(2):
                p, q, r = (b, d, a) if back else (d, a, b)
                pairs.append((4 * a + 2 * b + d, 4 * p + 2 * q + r))
    return lax.ppermute(value, ("zb", "c", "zh"), pairs)


def pick(value, index, axis=0):
    return lax.dynamic_index_in_dim(value, index, axis, keepdims=False)


def slot(value, index, count):
    here = lax.broadcasted_iota(jnp.int32, (count, 1), 0) == index
    return jnp.where(here, value[None], jnp.zeros((), value.dtype)).reshape(-1)


def arrange_kernel(info_ref, own_ref, other_ref, out_ref):
    count, tokens, heads = own_ref.shape
    own_at = pl.multiple_of(info_ref[count] * heads, heads)
    other_at = pl.multiple_of((1 - info_ref[count]) * heads, heads)
    for i in range(count):
        at = info_ref[i]
        span = slice(i * tokens, (i + 1) * tokens)
        out_ref[pl.ds(own_at, heads), span] = own_ref[at].T
        out_ref[pl.ds(other_at, heads), span] = other_ref[at].T


def grad_kernel(ctx_ref, *refs):
    blocks, (keep_ref, send_ref) = refs[:-2], refs[-2:]
    tile = jnp.concatenate([ref[...] for ref in blocks], axis=0)
    got = jnp.dot(ctx_ref[...], tile, preferred_element_type=jnp.float32)
    rows, cols = keep_ref.shape[2:]
    for k in range(keep_ref.shape[0]):
        span = slice(k * cols, (k + 1) * cols)
        send_ref[k, 0] = got[:rows, span].astype(send_ref.dtype)
        keep_ref[k, 0] = got[rows:, span]


def back_kernel(info_ref, *refs):
    y_count = SIZE["y"]
    mine_refs, came_refs = refs[:y_count], refs[y_count : 2 * y_count]
    blocks, (own_ref, other_ref, acc_ref) = refs[2 * y_count : -3], refs[-3:]
    count, tokens, heads = own_ref.shape
    step = pl.program_id(0)
    first = info_ref[count + 3] == 0
    rows = []
    for mine_ref, came_ref in zip(mine_refs, came_refs):
        mine, came = mine_ref[0], came_ref[0]
        rows += [jnp.where(first, mine, came), jnp.where(first, came, mine)]
    tile = jnp.concatenate([ref[...] for ref in blocks], axis=0)
    got = jnp.dot(tile, jnp.concatenate(rows, axis=0), preferred_element_type=jnp.float32)

    @pl.when(step == 0)
    def _():
        acc_ref[...] = got

    @pl.when(step > 0)
    def _():
        acc_ref[...] += got

    @pl.when(step == pl.num_programs(0) - 1)
    def _():
        straight = info_ref[count + 4] == 0
        for i in range(count):
            at = info_ref[i]
            left = acc_ref[i * tokens : (i + 1) * tokens, :heads]
            right = acc_ref[i * tokens : (i + 1) * tokens, heads:]
            own_ref[at] = jnp.where(straight, left, right)
            other_ref[at] = jnp.where(straight, right, left).astype(other_ref.dtype)


def total_kernel(mine_ref, *refs):
    came, out_ref = refs[:-1], refs[-1]
    cols = out_ref.shape[1]
    for za in range(2):
        total = mine_ref[za]
        for ref in came:
            total = total + ref[za].astype(jnp.float32)
        turned = total.T
        for zb in range(2):
            out_ref[2 * zb + za] = turned[zb * cols : (zb + 1) * cols]


def arrange(info, own, other):
    count, tokens, heads = own.shape
    full = pl.BlockSpec(own.shape, lambda i, p: (0, 0, 0))
    return pl.pallas_call(
        arrange_kernel,
        grid_spec=pltpu.PrefetchScalarGridSpec(
            num_scalar_prefetch=1,
            grid=(1,),
            in_specs=[full, full],
            out_specs=pl.BlockSpec((2 * heads, count * tokens), lambda i, p: (0, 0)),
        ),
        out_shape=jax.ShapeDtypeStruct((2 * heads, count * tokens), own.dtype),
        name="arrange",
    )(info, own, other)


def grad_of(ctx, blocks):
    twice, rows_in = ctx.shape
    tokens, half = blocks[0].shape
    tile = half // SIZE["za"]
    shape = (SIZE["y"], SIZE["za"], twice // 2, tile // SIZE["y"])
    out = pl.BlockSpec((SIZE["y"], 1) + shape[2:], lambda t: (0, t, 0, 0))
    return pl.pallas_call(
        grad_kernel,
        grid=(half // tile,),
        in_specs=[pl.BlockSpec(ctx.shape, lambda t: (0, 0))]
        + [pl.BlockSpec((tokens, tile), lambda t: (0, t))] * len(blocks),
        out_specs=[out, out],
        out_shape=[
            jax.ShapeDtypeStruct(shape, jnp.float32),
            jax.ShapeDtypeStruct(shape, jnp.bfloat16),
        ],
        cost_estimate=pl.CostEstimate(
            flops=2 * twice * rows_in * half, transcendentals=0, bytes_accessed=9 << 20
        ),
        name="grad",
    )(ctx, *blocks)


def back_of(info, mine, came, blocks):
    _, cols, twice = mine.shape
    tokens, half = blocks[0].shape
    count = len(blocks)
    tile = half // SIZE["za"]
    shape = (count, tokens, twice // 2)
    full = pl.BlockSpec(shape, lambda k, p: (0, 0, 0))

    def weights(place):
        def index(k, p):
            z = k ^ p[count + 1]
            y = place ^ p[count + 2]
            return (z * 8 + (y & 1) * 4 + ((y >> 1) & 1) * 2 + ((y >> 2) & 1), 0, 0)

        return pl.BlockSpec((1, cols, twice), index)

    return pl.pallas_call(
        back_kernel,
        grid_spec=pltpu.PrefetchScalarGridSpec(
            num_scalar_prefetch=1,
            grid=(half // tile,),
            in_specs=[weights(y) for y in range(SIZE["y"])] * 2
            + [pl.BlockSpec((tokens, tile), lambda k, p: (0, k))] * count,
            out_specs=[full, full],
            scratch_shapes=[pltpu.VMEM((count * tokens, twice), jnp.float32)],
        ),
        out_shape=[
            jax.ShapeDtypeStruct(shape, jnp.float32),
            jax.ShapeDtypeStruct(shape, jnp.bfloat16),
        ],
        cost_estimate=pl.CostEstimate(
            flops=2 * twice * count * tokens * half, transcendentals=0, bytes_accessed=8 << 20
        ),
        name="back",
    )(info, *([mine] * SIZE["y"] + [came] * SIZE["y"]), *blocks)


def total_of(mine, came, cols):
    return pl.pallas_call(
        total_kernel,
        out_shape=jax.ShapeDtypeStruct((4, cols, mine.shape[1]), jnp.float32),
        name="total",
    )(mine, *came)


def per_device(context, cotangent, lengths, weight, row_stat, col_stat):
    groups = SIZE["zb"] * SIZE["za"] * SIZE["y"] * SIZE["c"]
    zb, za, y, c, x, zh = (lax.axis_index(name) for name, _ in SPLIT)
    seq_here = lengths.shape[0]
    tokens, width = cotangent.shape
    target_len = tokens // seq_here
    heads = context.shape[1]
    half = width // 2
    cols = width // groups
    position = jnp.arange(target_len, dtype=jnp.int32)
    inside = position[None, :] < lengths[:, None]
    shaped = cotangent.reshape(seq_here, target_len, width)
    masked = jnp.where(inside[:, :, None], shaped, jnp.zeros((), cotangent.dtype)).reshape(
        tokens, width
    )

    left, right = masked[:, :half], masked[:, half:]
    theirs = flip(jnp.where(zh == 0, right, left), "zh")
    mine = jnp.where(zh == 0, left, right)
    blocks = [mine] + [shift(mine, "x", s) for s in X_STEPS]
    blocks += [theirs] + [shift(theirs, "x", s) for s in X_STEPS]
    info = [((x - s) & (SIZE["x"] - 1)) * 2 + z for z in (zh, 1 - zh) for s in (0,) + X_STEPS]
    info = jnp.stack(info + [1 - (c ^ zh), za, y, c, zb ^ zh]).astype(jnp.int32)
    context_other = flip(context, "zh")
    by_block = (len(blocks), tokens, heads)
    ctx = arrange(info, context.reshape(by_block), context_other.reshape(by_block))

    w = weight.T.astype(jnp.bfloat16)[None]
    for bit in (2, 1, 0):
        other = flip(w, "y", 1 << bit)
        w = jnp.concatenate([w, other], axis=0)
    w_a = turn(w, lambda a, b: (b, a))
    w_b = turn(w, lambda a, b: (1 - b, a))
    w = jnp.concatenate([w_a, w_b], axis=2)
    other = flip(w, "za")
    w = jnp.concatenate([w, other], axis=0)
    w_came = flip(w, "c")

    stats = rotate(jnp.concatenate([row_stat, col_stat]), True)
    row_held, col_held = stats[:heads], stats[heads:]

    kept, sent = grad_of(ctx, blocks)
    parts = kept + flip(sent, "c").astype(jnp.float32)

    own, other = back_of(info, w, w_came, blocks)
    context_grad = (own + flip(other, "zh").astype(jnp.float32)).astype(jnp.bfloat16)
    context_grad = context_grad.reshape(context.shape)

    narrow = parts.astype(jnp.bfloat16)
    last = SIZE["y"] - 1
    came = [shift(pick(narrow, (y + s) & last), "y", s) for s in Y_STEPS]
    pieces = total_of(pick(parts, y), came, cols)
    zl = zb * 2 + za
    part = pick(pieces, zl)
    for s in Z_STEPS:
        part = part + shift(pick(pieces, (zl + s) & 3), ("zb", "za"), s)
    grad = part / groups
    grad_own = rotate(grad, False)

    square = grad * grad + square_eps
    inner_total = heads * SIZE["x"] * SIZE["zh"]
    col_all = lax.psum(jnp.sum(square, axis=1), "c")
    col_all = lax.psum(col_all, "x")
    col_here = decay_rate * col_held + (1.0 - decay_rate) * (col_all / inner_total)
    scaled = grad * grad / col_here[:, None]
    rows = jnp.concatenate([jnp.sum(square, axis=0), jnp.sum(scaled, axis=0)])
    rows = lax.psum(rows, "y")
    rows = lax.psum(jnp.concatenate([rows, slot(col_here, zl, 4)]), ("zb", "za"))
    slots = slot(rows[2 * heads :], zh, 2)
    rows = lax.psum(jnp.concatenate([rows[: 2 * heads], slots]), "zh")
    slots = rows[2 * heads :].reshape(8, cols)
    col_new = pick(slots, zb * 4 + c * 2 + za)
    row_here = decay_rate * row_held + (1.0 - decay_rate) * (rows[:heads] / width)
    square_sum = jnp.sum(rows[heads : 2 * heads] / row_here)
    tail = jnp.broadcast_to(square_sum, (128,))
    sums = lax.psum(jnp.concatenate([slot(row_here, c, 2), tail]), "c")
    row_new = pick(sums[: 2 * heads].reshape(2, heads), zh)
    square_sum = lax.psum(sums[2 * heads], "x")
    raw_update = grad_own / jnp.sqrt(row_new[None, :] * col_new[:, None])
    update_rms = jnp.sqrt(square_sum / (inner_total * width))
    update = (raw_update / jnp.maximum(1.0, update_rms)).T
    return (context_grad, update, row_new, col_new)


def solution(mesh):
    names = tuple(name for name, _ in SPLIT)
    fine = Mesh(mesh.devices.reshape(tuple(size for _, size in SPLIT)), names)
    in_specs = (P(DP, MP), P(DP + MP, None), P(DP + MP), P(MP, DP), P(MP), P(DP))
    out_specs = (P(DP, MP), P(MP, DP), P(MP), P(DP))
    return jax.shard_map(
        per_device, mesh=fine, in_specs=in_specs, out_specs=out_specs, check_vma=False
    )
```

```python
import jax
import jax.numpy as jnp
from jax import lax
from jax.experimental import pallas as pl
from jax.experimental.pallas import tpu as pltpu
from jax.sharding import Mesh, PartitionSpec as P


decay_rate = 0.9
square_eps = 1e-30

SPLIT = (("zb", 2), ("za", 2), ("y", 8), ("c", 2), ("x", 4), ("zh", 2))
SIZE = dict(SPLIT)
DP = ("zb", "za", "y", "c")
MP = ("x", "zh")
X_STEPS = (1, 3, 2)
Z_STEPS = (2, 1, 3)


def shift(value, axes, step):
    size = 4 if axes == ("zb", "za") else SIZE[axes]
    return lax.ppermute(value, axes, [(i, (i + step) % size) for i in range(size)])


def flip(value, axis, mask=1):
    return lax.ppermute(value, axis, [(i, i ^ mask) for i in range(SIZE[axis])])


def turn(value, to):
    pairs = []
    for a in range(2):
        for b in range(2):
            p, q = to(a, b)
            pairs.append((2 * a + b, 2 * p + q))
    return lax.ppermute(value, ("zb", "zh"), pairs)


def rotate(value, back):
    pairs = []
    for a in range(2):
        for b in range(2):
            for d in range(2):
                p, q, r = (b, d, a) if back else (d, a, b)
                pairs.append((4 * a + 2 * b + d, 4 * p + 2 * q + r))
    return lax.ppermute(value, ("zb", "c", "zh"), pairs)


def pick(value, index, axis=0):
    return lax.dynamic_index_in_dim(value, index, axis, keepdims=False)


def slot(value, index, count):
    here = lax.broadcasted_iota(jnp.int32, (count, 1), 0) == index
    return jnp.where(here, value[None], jnp.zeros((), value.dtype)).reshape(-1)


def arrange_kernel(info_ref, own_ref, other_ref, out_ref):
    count, tokens, heads = own_ref.shape
    own_at = pl.multiple_of(info_ref[count] * heads, heads)
    other_at = pl.multiple_of((1 - info_ref[count]) * heads, heads)
    for i in range(count):
        at = info_ref[i]
        span = slice(i * tokens, (i + 1) * tokens)
        out_ref[pl.ds(own_at, heads), span] = own_ref[at].T
        out_ref[pl.ds(other_at, heads), span] = other_ref[at].T


def grad_kernel(ctx_ref, *refs):
    blocks, (keep_ref, send_ref) = refs[:-2], refs[-2:]
    tile = jnp.concatenate([ref[...] for ref in blocks], axis=0)
    got = jnp.dot(ctx_ref[...], tile, preferred_element_type=jnp.float32)
    rows, cols = keep_ref.shape[2:]
    for k in range(keep_ref.shape[0]):
        span = slice(k * cols, (k + 1) * cols)
        send_ref[k, 0] = got[:rows, span].astype(send_ref.dtype)
        keep_ref[k, 0] = got[rows:, span]


def back_kernel(info_ref, *refs):
    y_count = SIZE["y"]
    mine_refs, came_refs = refs[:y_count], refs[y_count : 2 * y_count]
    blocks, (own_ref, other_ref, acc_ref) = refs[2 * y_count : -3], refs[-3:]
    count, tokens, heads = own_ref.shape
    step = pl.program_id(0)
    first = info_ref[count + 3] == 0
    rows = []
    for mine_ref, came_ref in zip(mine_refs, came_refs):
        mine, came = mine_ref[0], came_ref[0]
        rows += [jnp.where(first, mine, came), jnp.where(first, came, mine)]
    tile = jnp.concatenate([ref[...] for ref in blocks], axis=0)
    got = jnp.dot(tile, jnp.concatenate(rows, axis=0), preferred_element_type=jnp.float32)

    @pl.when(step == 0)
    def _():
        acc_ref[...] = got

    @pl.when(step > 0)
    def _():
        acc_ref[...] += got

    @pl.when(step == pl.num_programs(0) - 1)
    def _():
        straight = info_ref[count + 4] == 0
        for i in range(count):
            at = info_ref[i]
            left = acc_ref[i * tokens : (i + 1) * tokens, :heads]
            right = acc_ref[i * tokens : (i + 1) * tokens, heads:]
            own_ref[at] = jnp.where(straight, left, right)
            other_ref[at] = jnp.where(straight, right, left).astype(other_ref.dtype)


def total_kernel(info_ref, kept_ref, swapped_ref, came_ref, *refs):
    out_refs, pieces_ref = refs[:4], refs[4]
    y_count, za_count, _, wide = came_ref.shape
    cols = wide // 2
    here = info_ref[0]
    for za in range(za_count):
        total = kept_ref[0, za] + swapped_ref[0, za].astype(jnp.float32)
        for i in range(y_count):
            part = came_ref[i, za].astype(jnp.float32)
            total = total + jnp.where(here == i, jnp.zeros_like(part), part)
        turned = total.T
        for zb in range(2):
            pieces_ref[2 * zb + za] = turned[zb * cols : (zb + 1) * cols]
    for i, s in enumerate((0,) + Z_STEPS):
        out_refs[i][...] = pieces_ref[(info_ref[1] + s) & 3]


def arrange(info, own, other):
    count, tokens, heads = own.shape
    full = pl.BlockSpec(own.shape, lambda i, p: (0, 0, 0))
    return pl.pallas_call(
        arrange_kernel,
        grid_spec=pltpu.PrefetchScalarGridSpec(
            num_scalar_prefetch=1,
            grid=(1,),
            in_specs=[full, full],
            out_specs=pl.BlockSpec((2 * heads, count * tokens), lambda i, p: (0, 0)),
        ),
        out_shape=jax.ShapeDtypeStruct((2 * heads, count * tokens), own.dtype),
        name="arrange",
    )(info, own, other)


def grad_of(ctx, blocks):
    twice, rows_in = ctx.shape
    tokens, half = blocks[0].shape
    tile = half // SIZE["za"]
    shape = (SIZE["y"], SIZE["za"], twice // 2, tile // SIZE["y"])
    out = pl.BlockSpec((SIZE["y"], 1) + shape[2:], lambda t: (0, t, 0, 0))
    return pl.pallas_call(
        grad_kernel,
        grid=(half // tile,),
        in_specs=[pl.BlockSpec(ctx.shape, lambda t: (0, 0))]
        + [pl.BlockSpec((tokens, tile), lambda t: (0, t))] * len(blocks),
        out_specs=[out, out],
        out_shape=[
            jax.ShapeDtypeStruct(shape, jnp.float32),
            jax.ShapeDtypeStruct(shape, jnp.bfloat16),
        ],
        cost_estimate=pl.CostEstimate(
            flops=2 * twice * rows_in * half, transcendentals=0, bytes_accessed=9 << 20
        ),
        name="grad",
    )(ctx, *blocks)


def back_of(info, mine, came, blocks):
    _, cols, twice = mine.shape
    tokens, half = blocks[0].shape
    count = len(blocks)
    tile = half // SIZE["za"]
    shape = (count, tokens, twice // 2)
    full = pl.BlockSpec(shape, lambda k, p: (0, 0, 0))

    def weights(place):
        def index(k, p):
            z = k ^ p[count + 1]
            y = place ^ p[count + 2]
            return (z * 8 + (y & 1) * 4 + ((y >> 1) & 1) * 2 + ((y >> 2) & 1), 0, 0)

        return pl.BlockSpec((1, cols, twice), index)

    return pl.pallas_call(
        back_kernel,
        grid_spec=pltpu.PrefetchScalarGridSpec(
            num_scalar_prefetch=1,
            grid=(half // tile,),
            in_specs=[weights(y) for y in range(SIZE["y"])] * 2
            + [pl.BlockSpec((tokens, tile), lambda k, p: (0, k))] * count,
            out_specs=[full, full],
            scratch_shapes=[pltpu.VMEM((count * tokens, twice), jnp.float32)],
        ),
        out_shape=[
            jax.ShapeDtypeStruct(shape, jnp.float32),
            jax.ShapeDtypeStruct(shape, jnp.bfloat16),
        ],
        cost_estimate=pl.CostEstimate(
            flops=2 * twice * count * tokens * half, transcendentals=0, bytes_accessed=8 << 20
        ),
        name="back",
    )(info, *([mine] * SIZE["y"] + [came] * SIZE["y"]), *blocks)


def total_of(info, kept, swapped, came):
    _, za_count, rows, wide = came.shape
    piece = (wide // 2, rows)
    own = pl.BlockSpec((1, za_count, rows, wide), lambda i, p: (p[0], 0, 0, 0))
    full = pl.BlockSpec(came.shape, lambda i, p: (0, 0, 0, 0))
    return pl.pallas_call(
        total_kernel,
        grid_spec=pltpu.PrefetchScalarGridSpec(
            num_scalar_prefetch=1,
            grid=(1,),
            in_specs=[own, own, full],
            out_specs=[pl.BlockSpec(piece, lambda i, p: (0, 0))] * 4,
            scratch_shapes=[pltpu.VMEM((4,) + piece, jnp.float32)],
        ),
        out_shape=[jax.ShapeDtypeStruct(piece, jnp.float32)] * 4,
        name="total",
    )(info, kept, swapped, came)


def per_device(context, cotangent, lengths, weight, row_stat, col_stat):
    groups = SIZE["zb"] * SIZE["za"] * SIZE["y"] * SIZE["c"]
    zb, za, y, c, x, zh = (lax.axis_index(name) for name, _ in SPLIT)
    seq_here = lengths.shape[0]
    tokens, width = cotangent.shape
    target_len = tokens // seq_here
    heads = context.shape[1]
    half = width // 2
    cols = width // groups
    position = jnp.arange(target_len, dtype=jnp.int32)
    inside = position[None, :] < lengths[:, None]
    shaped = cotangent.reshape(seq_here, target_len, width)
    masked = jnp.where(inside[:, :, None], shaped, jnp.zeros((), cotangent.dtype)).reshape(
        tokens, width
    )

    left, right = masked[:, :half], masked[:, half:]
    theirs = flip(jnp.where(zh == 0, right, left), "zh")
    mine = jnp.where(zh == 0, left, right)
    blocks = [mine] + [shift(mine, "x", s) for s in X_STEPS]
    blocks += [theirs] + [shift(theirs, "x", s) for s in X_STEPS]
    info = [((x - s) & (SIZE["x"] - 1)) * 2 + z for z in (zh, 1 - zh) for s in (0,) + X_STEPS]
    info = jnp.stack(info + [1 - (c ^ zh), za, y, c, zb ^ zh]).astype(jnp.int32)
    context_other = flip(context, "zh")
    by_block = (len(blocks), tokens, heads)
    ctx = arrange(info, context.reshape(by_block), context_other.reshape(by_block))

    w = weight.T.astype(jnp.bfloat16)[None]
    for bit in (2, 1, 0):
        other = flip(w, "y", 1 << bit)
        w = jnp.concatenate([w, other], axis=0)
    w_a = turn(w, lambda a, b: (b, a))
    w_b = turn(w, lambda a, b: (1 - b, a))
    w = jnp.concatenate([w_a, w_b], axis=2)
    other = flip(w, "za")
    w = jnp.concatenate([w, other], axis=0)
    w_came = flip(w, "c")

    stats = rotate(jnp.concatenate([row_stat, col_stat]), True)
    row_held, col_held = stats[:heads], stats[heads:]

    kept, sent = grad_of(ctx, blocks)
    swapped = flip(sent, "c")
    narrow = (kept + swapped.astype(jnp.float32)).astype(jnp.bfloat16)

    own, other = back_of(info, w, w_came, blocks)
    came = flip(other, "zh")
    context_grad = (own + came.astype(jnp.float32)).astype(jnp.bfloat16)
    context_grad = context_grad.reshape(context.shape)

    came = lax.all_to_all(narrow, "y", 0, 0, tiled=True)
    zl = zb * 2 + za
    part, *pieces = total_of(jnp.stack([y, zl]).astype(jnp.int32), kept, swapped, came)
    for i, s in enumerate(Z_STEPS):
        part = part + shift(pieces[i], ("zb", "za"), s)
    grad = part / groups
    grad_own = rotate(grad, False)

    square = grad * grad + square_eps
    inner_total = heads * SIZE["x"] * SIZE["zh"]
    col_all = lax.psum(jnp.sum(square, axis=1), "c")
    col_all = lax.psum(col_all, "x")
    col_here = decay_rate * col_held + (1.0 - decay_rate) * (col_all / inner_total)
    scaled = grad * grad / col_here[:, None]
    rows = jnp.concatenate([jnp.sum(square, axis=0), jnp.sum(scaled, axis=0)])
    rows = lax.psum(rows, "y")
    rows = lax.psum(jnp.concatenate([rows, slot(col_here, zl, 4)]), ("zb", "za"))
    slots = slot(rows[2 * heads :], zh, 2)
    rows = lax.psum(jnp.concatenate([rows[: 2 * heads], slots]), "zh")
    slots = rows[2 * heads :].reshape(8, cols)
    col_new = pick(slots, zb * 4 + c * 2 + za)
    row_here = decay_rate * row_held + (1.0 - decay_rate) * (rows[:heads] / width)
    square_sum = jnp.sum(rows[heads : 2 * heads] / row_here)
    tail = jnp.broadcast_to(square_sum, (128,))
    sums = lax.psum(jnp.concatenate([slot(row_here, c, 2), tail]), "c")
    row_new = pick(sums[: 2 * heads].reshape(2, heads), zh)
    square_sum = lax.psum(sums[2 * heads], "x")
    raw_update = grad_own / jnp.sqrt(row_new[None, :] * col_new[:, None])
    update_rms = jnp.sqrt(square_sum / (inner_total * width))
    update = (raw_update / jnp.maximum(1.0, update_rms)).T
    return (context_grad, update, row_new, col_new)


def solution(mesh):
    names = tuple(name for name, _ in SPLIT)
    fine = Mesh(mesh.devices.reshape(tuple(size for _, size in SPLIT)), names)
    in_specs = (P(DP, MP), P(DP + MP, None), P(DP + MP), P(MP, DP), P(MP), P(DP))
    out_specs = (P(DP, MP), P(MP, DP), P(MP), P(DP))
    return jax.shard_map(
        per_device, mesh=fine, in_specs=in_specs, out_specs=out_specs, check_vma=False
    )
```

```python
import jax
import jax.numpy as jnp
from jax import lax
from jax.experimental import pallas as pl
from jax.experimental.pallas import tpu as pltpu
from jax.sharding import Mesh, PartitionSpec as P


decay_rate = 0.9
square_eps = 1e-30

SPLIT = (("zb", 2), ("za", 2), ("y", 8), ("c", 2), ("x", 4), ("zh", 2))
SIZE = dict(SPLIT)
DP = ("zb", "za", "y", "c")
MP = ("x", "zh")
X_STEPS = (1, 3, 2)


def shift(value, axis, step):
    size = SIZE[axis]
    return lax.ppermute(value, axis, [(i, (i + step) % size) for i in range(size)])


def flip(value, axis, mask=1):
    return lax.ppermute(value, axis, [(i, i ^ mask) for i in range(SIZE[axis])])


def turn(value, to):
    pairs = []
    for a in range(2):
        for b in range(2):
            p, q = to(a, b)
            pairs.append((2 * a + b, 2 * p + q))
    return lax.ppermute(value, ("zb", "zh"), pairs)


def rotate(value, back):
    pairs = []
    for a in range(2):
        for b in range(2):
            for d in range(2):
                p, q, r = (b, d, a) if back else (d, a, b)
                pairs.append((4 * a + 2 * b + d, 4 * p + 2 * q + r))
    return lax.ppermute(value, ("zb", "c", "zh"), pairs)


def pick(value, index, axis=0):
    return lax.dynamic_index_in_dim(value, index, axis, keepdims=False)


def slot(value, index, count):
    here = lax.broadcasted_iota(jnp.int32, (count, 1), 0) == index
    return jnp.where(here, value[None], jnp.zeros((), value.dtype)).reshape(-1)


def arrange_kernel(info_ref, own_ref, other_ref, out_ref):
    count, tokens, heads = own_ref.shape
    own_at = pl.multiple_of(info_ref[count] * heads, heads)
    other_at = pl.multiple_of((1 - info_ref[count]) * heads, heads)
    for i in range(count):
        at = info_ref[i]
        span = slice(i * tokens, (i + 1) * tokens)
        out_ref[pl.ds(own_at, heads), span] = own_ref[at].T
        out_ref[pl.ds(other_at, heads), span] = other_ref[at].T


def grad_kernel(ctx_ref, *refs):
    blocks, (keep_ref, send_ref) = refs[:-2], refs[-2:]
    tile = jnp.concatenate([ref[...] for ref in blocks], axis=0)
    got = jnp.dot(ctx_ref[...], tile, preferred_element_type=jnp.float32)
    rows, cols = keep_ref.shape[2:]
    for k in range(keep_ref.shape[0]):
        span = slice(k * cols, (k + 1) * cols)
        send_ref[k, 0] = got[:rows, span].astype(send_ref.dtype)
        keep_ref[k, 0] = got[rows:, span]


def back_kernel(info_ref, *refs):
    y_count = SIZE["y"]
    mine_refs, came_refs = refs[:y_count], refs[y_count : 2 * y_count]
    blocks, (own_ref, other_ref, acc_ref) = refs[2 * y_count : -3], refs[-3:]
    count, tokens, heads = own_ref.shape
    step = pl.program_id(0)
    first = info_ref[count + 3] == 0
    rows = []
    for mine_ref, came_ref in zip(mine_refs, came_refs):
        mine, came = mine_ref[0], came_ref[0]
        rows += [jnp.where(first, mine, came), jnp.where(first, came, mine)]
    tile = jnp.concatenate([ref[...] for ref in blocks], axis=0)
    got = jnp.dot(tile, jnp.concatenate(rows, axis=0), preferred_element_type=jnp.float32)

    @pl.when(step == 0)
    def _():
        acc_ref[...] = got

    @pl.when(step > 0)
    def _():
        acc_ref[...] += got

    @pl.when(step == pl.num_programs(0) - 1)
    def _():
        straight = info_ref[count + 4] == 0
        for i in range(count):
            at = info_ref[i]
            left = acc_ref[i * tokens : (i + 1) * tokens, :heads]
            right = acc_ref[i * tokens : (i + 1) * tokens, heads:]
            own_ref[at] = jnp.where(straight, left, right)
            other_ref[at] = jnp.where(straight, right, left).astype(other_ref.dtype)


def total_kernel(info_ref, kept_ref, swapped_ref, came_ref, out_ref):
    y_count, za_count, _, wide = came_ref.shape
    cols = wide // 2
    here = info_ref[0]
    for za in range(za_count):
        total = kept_ref[za] + swapped_ref[za].astype(jnp.float32)
        for i in range(y_count):
            part = came_ref[i, za].astype(jnp.float32)
            total = total + jnp.where(here == i, jnp.zeros_like(part), part)
        turned = total.T
        for zb in range(2):
            out_ref[2 * zb + za] = turned[zb * cols : (zb + 1) * cols]


def arrange(info, own, other):
    count, tokens, heads = own.shape
    full = pl.BlockSpec(own.shape, lambda i, p: (0, 0, 0))
    return pl.pallas_call(
        arrange_kernel,
        grid_spec=pltpu.PrefetchScalarGridSpec(
            num_scalar_prefetch=1,
            grid=(1,),
            in_specs=[full, full],
            out_specs=pl.BlockSpec((2 * heads, count * tokens), lambda i, p: (0, 0)),
        ),
        out_shape=jax.ShapeDtypeStruct((2 * heads, count * tokens), own.dtype),
        name="arrange",
    )(info, own, other)


def grad_of(ctx, blocks):
    twice, rows_in = ctx.shape
    tokens, half = blocks[0].shape
    tile = half // SIZE["za"]
    shape = (SIZE["y"], SIZE["za"], twice // 2, tile // SIZE["y"])
    out = pl.BlockSpec((SIZE["y"], 1) + shape[2:], lambda t: (0, t, 0, 0))
    return pl.pallas_call(
        grad_kernel,
        grid=(half // tile,),
        in_specs=[pl.BlockSpec(ctx.shape, lambda t: (0, 0))]
        + [pl.BlockSpec((tokens, tile), lambda t: (0, t))] * len(blocks),
        out_specs=[out, out],
        out_shape=[
            jax.ShapeDtypeStruct(shape, jnp.float32),
            jax.ShapeDtypeStruct(shape, jnp.bfloat16),
        ],
        cost_estimate=pl.CostEstimate(
            flops=2 * twice * rows_in * half, transcendentals=0, bytes_accessed=9 << 20
        ),
        name="grad",
    )(ctx, *blocks)


def back_of(info, mine, came, blocks):
    _, cols, twice = mine.shape
    tokens, half = blocks[0].shape
    count = len(blocks)
    tile = half // SIZE["za"]
    shape = (count, tokens, twice // 2)
    full = pl.BlockSpec(shape, lambda k, p: (0, 0, 0))

    def weights(place):
        def index(k, p):
            z = k ^ p[count + 1]
            y = place ^ p[count + 2]
            return (z * 8 + (y & 1) * 4 + ((y >> 1) & 1) * 2 + ((y >> 2) & 1), 0, 0)

        return pl.BlockSpec((1, cols, twice), index)

    return pl.pallas_call(
        back_kernel,
        grid_spec=pltpu.PrefetchScalarGridSpec(
            num_scalar_prefetch=1,
            grid=(half // tile,),
            in_specs=[weights(y) for y in range(SIZE["y"])] * 2
            + [pl.BlockSpec((tokens, tile), lambda k, p: (0, k))] * count,
            out_specs=[full, full],
            scratch_shapes=[pltpu.VMEM((count * tokens, twice), jnp.float32)],
        ),
        out_shape=[
            jax.ShapeDtypeStruct(shape, jnp.float32),
            jax.ShapeDtypeStruct(shape, jnp.bfloat16),
        ],
        cost_estimate=pl.CostEstimate(
            flops=2 * twice * count * tokens * half, transcendentals=0, bytes_accessed=8 << 20
        ),
        name="back",
    )(info, *([mine] * SIZE["y"] + [came] * SIZE["y"]), *blocks)


def total_of(info, kept, swapped, came):
    _, za_count, rows, wide = came.shape
    out = (2 * za_count, wide // 2, rows)
    whole = pl.BlockSpec(memory_space=pltpu.VMEM)
    return pl.pallas_call(
        total_kernel,
        in_specs=[pl.BlockSpec(memory_space=pltpu.SMEM), whole, whole, whole],
        out_specs=whole,
        out_shape=jax.ShapeDtypeStruct(out, jnp.float32),
        name="total",
    )(info, kept, swapped, came)


def per_device(context, cotangent, lengths, weight, row_stat, col_stat):
    groups = SIZE["zb"] * SIZE["za"] * SIZE["y"] * SIZE["c"]
    zb, za, y, c, x, zh = (lax.axis_index(name) for name, _ in SPLIT)
    seq_here = lengths.shape[0]
    tokens, width = cotangent.shape
    target_len = tokens // seq_here
    heads = context.shape[1]
    half = width // 2
    cols = width // groups
    position = jnp.arange(target_len, dtype=jnp.int32)
    inside = position[None, :] < lengths[:, None]
    shaped = cotangent.reshape(seq_here, target_len, width)
    masked = jnp.where(inside[:, :, None], shaped, jnp.zeros((), cotangent.dtype)).reshape(
        tokens, width
    )

    left, right = masked[:, :half], masked[:, half:]
    theirs = flip(jnp.where(zh == 0, right, left), "zh")
    mine = jnp.where(zh == 0, left, right)
    blocks = [mine] + [shift(mine, "x", s) for s in X_STEPS]
    blocks += [theirs] + [shift(theirs, "x", s) for s in X_STEPS]
    info = [((x - s) & (SIZE["x"] - 1)) * 2 + z for z in (zh, 1 - zh) for s in (0,) + X_STEPS]
    info = jnp.stack(info + [1 - (c ^ zh), za, y, c, zb ^ zh]).astype(jnp.int32)
    context_other = flip(context, "zh")
    by_block = (len(blocks), tokens, heads)
    ctx = arrange(info, context.reshape(by_block), context_other.reshape(by_block))

    w = weight.T.astype(jnp.bfloat16)[None]
    for bit in (2, 1, 0):
        other = flip(w, "y", 1 << bit)
        w = jnp.concatenate([w, other], axis=0)
    w_a = turn(w, lambda a, b: (b, a))
    w_b = turn(w, lambda a, b: (1 - b, a))
    w = jnp.concatenate([w_a, w_b], axis=2)
    other = flip(w, "za")
    w = jnp.concatenate([w, other], axis=0)
    w_came = flip(w, "c")

    stats = rotate(jnp.concatenate([row_stat, col_stat]), True)
    row_held, col_held = stats[:heads], stats[heads:]

    kept, sent = grad_of(ctx, blocks)
    swapped = flip(sent, "c")
    narrow = (kept + swapped.astype(jnp.float32)).astype(jnp.bfloat16)

    own, other = back_of(info, w, w_came, blocks)
    came = flip(other, "zh")
    context_grad = (own + came.astype(jnp.float32)).astype(jnp.bfloat16)
    context_grad = context_grad.reshape(context.shape)

    came = lax.all_to_all(narrow, "y", 0, 0, tiled=True)
    zl = zb * 2 + za
    pieces = total_of(y.astype(jnp.int32)[None], pick(kept, y), pick(swapped, y), came)
    pieces = lax.all_to_all(pieces, ("zb", "za"), 0, 0, tiled=True)
    part = jnp.sum(pieces, axis=0)
    grad = part / groups
    grad_own = rotate(grad, False)

    square = grad * grad + square_eps
    inner_total = heads * SIZE["x"] * SIZE["zh"]
    col_all = lax.psum(jnp.sum(square, axis=1), "c")
    col_all = lax.psum(col_all, "x")
    col_here = decay_rate * col_held + (1.0 - decay_rate) * (col_all / inner_total)
    scaled = grad * grad / col_here[:, None]
    rows = jnp.concatenate([jnp.sum(square, axis=0), jnp.sum(scaled, axis=0)])
    rows = lax.psum(rows, "y")
    rows = lax.psum(jnp.concatenate([rows, slot(col_here, zl, 4)]), ("zb", "za"))
    slots = slot(rows[2 * heads :], zh, 2)
    rows = lax.psum(jnp.concatenate([rows[: 2 * heads], slots]), "zh")
    slots = rows[2 * heads :].reshape(8, cols)
    col_new = pick(slots, zb * 4 + c * 2 + za)
    row_here = decay_rate * row_held + (1.0 - decay_rate) * (rows[:heads] / width)
    square_sum = jnp.sum(rows[heads : 2 * heads] / row_here)
    tail = jnp.broadcast_to(square_sum, (128,))
    sums = lax.psum(jnp.concatenate([slot(row_here, c, 2), tail]), "c")
    row_new = pick(sums[: 2 * heads].reshape(2, heads), zh)
    square_sum = lax.psum(sums[2 * heads], "x")
    raw_update = grad_own / jnp.sqrt(row_new[None, :] * col_new[:, None])
    update_rms = jnp.sqrt(square_sum / (inner_total * width))
    update = (raw_update / jnp.maximum(1.0, update_rms)).T
    return (context_grad, update, row_new, col_new)


def solution(mesh):
    names = tuple(name for name, _ in SPLIT)
    fine = Mesh(mesh.devices.reshape(tuple(size for _, size in SPLIT)), names)
    in_specs = (P(DP, MP), P(DP + MP, None), P(DP + MP), P(MP, DP), P(MP), P(DP))
    out_specs = (P(DP, MP), P(MP, DP), P(MP), P(DP))
    return jax.shard_map(
        per_device, mesh=fine, in_specs=in_specs, out_specs=out_specs, check_vma=False
    )
```
